32 devices in a mesh: row: 4 (over z), col: 8 (over y, x, core).
Axes of the slice: x: 2, y: 2, z: 4, core: 2. Of those that a mesh axis runs over, the one named last changes fastest.
Arguments:
- pair: bfloat16 [256, 256, 128], P('row', 'col'), may hold values from -6 to 6
- grad_out: bfloat16 [256, 256, 128], P('row', 'col'), may hold values from -6 to 6
- keep: int32 [2, 2], replicated, may hold values from 0 to 1, as said below
- w_proj: bfloat16 [128, 512], replicated, may hold values from -0.5 to 0.5
- w_gate: bfloat16 [128, 128], replicated, may hold values from -0.5 to 0.5
- w_out: bfloat16 [128, 128], replicated, may hold values from -0.5 to 0.5
- gain_in: float32 [128], replicated, may hold values from 0.1 to 1.9
- gain_out: float32 [128], replicated, may hold values from 0.1 to 1.9
Outputs:
- grad_pair: bfloat16 [256, 256, 128], P('row', 'col')
The draws below stay inside these ranges and needn't reach their ends.
Inputs may be any that keep to these rules, and one draw needn't show every extreme that they name: keep[I, K] is 1 where residue blocks I and K of 128 residues form a kept pair; every diagonal block pair is kept and block pair (1, 0) never is.
All inputs are finite; a program needn't handle non-finite values.
Results may differ from the reference program's by a relative error of at most 0.02.
Values may be sent and summed in bfloat16 or wider, within the bound.
A program may use at most 128 MiB of HBM per device.

```python
import jax
import jax.numpy as jnp
from jax import lax

C = 128
BS = 128
L = 256
NB = 2


def draw_keep(key, part):
    key_rate = jax.random.fold_in(key, 11)
    key_cell = jax.random.fold_in(key, 23)
    thresholds = jax.random.randint(key_rate, (NB, 1), 20, 95)
    rolls = jax.random.randint(key_cell, (NB, NB), 0, 100)
    row_index = jnp.arange(NB)[:, None]
    col_index = jnp.arange(NB)[None, :]
    kept = (rolls < thresholds) | (row_index == col_index)
    barred = (row_index == NB - 1) & (col_index == 0)
    kept = kept & jnp.logical_not(barred)
    return kept.astype(jnp.int32)


def block_levels(stream_key, extent, cuts, smallest, largest):
    level = 1.0
    for position, shards_of in cuts:
        steps = jax.random.uniform(jax.random.fold_in(jax.random.fold_in(stream_key, 6), position), (shards_of,), jnp.float32, smallest / len(cuts), largest / len(cuts))
        level = level * jnp.repeat(jnp.exp(steps), extent[position] // shards_of).reshape((-1,) + (1,) * (len(extent) - 1 - position))
    return level


def normal_values(rng, extent, scale, bound, pieces=(), kind=jnp.bfloat16):
    array = jax.random.normal(rng, extent, jnp.float32) * scale
    if len(pieces) > 0:
        array = block_levels(rng, extent, pieces, -0.22, 0.18) * array
    return jnp.clip(array, min=-bound, max=bound).astype(kind)


def setup_inputs(seed: int = 0) -> dict:
    keys = jax.random.split(jax.random.key(seed), 9)
    return {
        "pair": normal_values(keys[0], (L, L, C), 1.0, 6.0, ((0, 4), (1, 8))),
        "grad_out": normal_values(keys[1], (L, L, C), 1.0, 6.0, ((0, 4), (1, 8))),
        "keep": draw_keep(jax.random.fold_in(keys[8], 71), 0),
        "w_proj": normal_values(keys[3], (C, 4 * C), C ** -0.5, 0.5),
        "w_gate": normal_values(keys[4], (C, C), C ** -0.5, 0.5),
        "w_out": normal_values(keys[5], (C, C), C ** -0.5, 0.5),
        "gain_in": jnp.clip(1.0 + 0.18 * jax.random.normal(keys[6], (C,), jnp.float32), 0.1, 1.9),
        "gain_out": jnp.clip(1.0 + 0.18 * jax.random.normal(keys[7], (C,), jnp.float32), 0.1, 1.9),
    }


def layer_norm(values, gain):
    means = lax.optimization_barrier(jnp.mean(values, -1, keepdims=True))
    centred = values - means
    inverse = jax.lax.rsqrt(lax.optimization_barrier(jnp.mean(centred * centred, -1, keepdims=True)) + 1e-05)
    scaled = centred * inverse
    return (scaled * gain, scaled, inverse)

def norm_back(upstream, gain, scaled, inverse):
    weighted = upstream * gain
    mean_one = lax.optimization_barrier(jnp.mean(weighted, -1, keepdims=True))
    mean_two = lax.optimization_barrier(jnp.mean(weighted * scaled, -1, keepdims=True))
    return inverse * (weighted - mean_one - scaled * mean_two)

def reference(pair, grad_out, keep, w_proj, w_gate, w_out, gain_in, gain_out):
    normed, scaled, inverse = layer_norm(pair.astype(jnp.float32), gain_in)
    normed_low = normed.astype(jnp.bfloat16)
    proj = jnp.dot(normed_low, w_proj, preferred_element_type=jnp.float32)
    part_zero, part_one, part_two, part_three = jnp.split(proj, 4, axis=-1)
    block_keep = jnp.repeat(jnp.repeat(keep, BS, axis=0), BS, axis=1)
    mask = block_keep.astype(jnp.float32)[:, :, None]
    sig_left = jax.nn.sigmoid(part_one)
    sig_right = jax.nn.sigmoid(part_three)
    left = (mask * sig_left * part_zero).astype(jnp.bfloat16)
    right = (mask * sig_right * part_two).astype(jnp.bfloat16)
    left_wide = left.astype(jnp.float32)
    right_wide = right.astype(jnp.float32)
    tri = jnp.einsum('ikc,jkc->ijc', left_wide, right_wide)
    tnorm, tri_hat, tri_inverse = layer_norm(tri, gain_out)
    tnorm_low = tnorm.astype(jnp.bfloat16)
    gate = jax.nn.sigmoid(jnp.dot(normed_low, w_gate, preferred_element_type=jnp.float32))
    proj_out = jnp.dot(tnorm_low, w_out, preferred_element_type=jnp.float32)
    upstream = grad_out.astype(jnp.float32)
    d_out = (upstream * gate).astype(jnp.bfloat16)
    d_gate = upstream * proj_out * gate * (1.0 - gate)
    d_tnorm = jnp.dot(d_out, w_out.T, preferred_element_type=jnp.float32)
    d_tri = norm_back(d_tnorm, gain_out, tri_hat, tri_inverse).astype(jnp.bfloat16)
    d_tri_wide = d_tri.astype(jnp.float32)
    d_left = jnp.einsum('ijc,jkc->ikc', d_tri_wide, right_wide)
    d_right = jnp.einsum('ijc,ikc->jkc', d_tri_wide, left_wide)
    d_zero = d_left * mask * sig_left
    d_one = d_left * mask * part_zero * sig_left * (1.0 - sig_left)
    d_two = d_right * mask * sig_right
    d_three = d_right * mask * part_two * sig_right * (1.0 - sig_right)
    d_all = jnp.concatenate([d_zero, d_one, d_two, d_three, d_gate], axis=-1).astype(jnp.bfloat16)
    w_back = jnp.concatenate([w_proj, w_gate], axis=1)
    d_normed = jnp.dot(d_all, w_back.T, preferred_element_type=jnp.float32)
    return norm_back(d_normed, gain_in, scaled, inverse).astype(jnp.bfloat16)
```

```python
import functools

import jax
import jax.numpy as jnp
from jax import lax
from jax.experimental import pallas as pl
from jax.experimental.pallas import tpu as pltpu
from jax.sharding import PartitionSpec as P

BS = 128


def layer_norm(values, gain):
    means = jnp.mean(values, -1, keepdims=True)
    centred = values - means
    inverse = lax.rsqrt(jnp.mean(centred * centred, -1, keepdims=True) + 1e-05)
    scaled = centred * inverse
    return (scaled * gain, scaled, inverse)


def norm_back(upstream, gain, scaled, inverse):
    weighted = upstream * gain
    mean_one = jnp.mean(weighted, -1, keepdims=True)
    mean_two = jnp.mean(weighted * scaled, -1, keepdims=True)
    return inverse * (weighted - mean_one - scaled * mean_two)


def block_mask(keep, row_start, row_count, col_start, col_count):
    block_ids = jnp.arange(keep.shape[0], dtype=jnp.int32)
    row_blocks = (row_start + jnp.arange(row_count, dtype=jnp.int32)) // BS
    col_blocks = (col_start + jnp.arange(col_count, dtype=jnp.int32)) // BS
    row_pick = (row_blocks[:, None] == block_ids[None, :]).astype(jnp.float32)
    col_pick = (col_blocks[:, None] == block_ids[None, :]).astype(jnp.float32)
    picked = jnp.dot(row_pick, keep.astype(jnp.float32))
    return jnp.dot(picked, col_pick.T)


def on_device(pair, grad_out, keep, w_proj, w_gate, w_out, gain_in, gain_out):
    rows_dev, cols_dev, chans = pair.shape
    normed, scaled, inverse = layer_norm(pair.astype(jnp.float32), gain_in)
    normed_low = normed.astype(jnp.bfloat16)
    proj = jnp.dot(normed_low, w_proj, preferred_element_type=jnp.float32)
    part_zero, part_one, part_two, part_three = jnp.split(proj, 4, axis=-1)
    row_first = lax.axis_index("row") * rows_dev
    col_first = lax.axis_index("col") * cols_dev
    mask = block_mask(keep, row_first, rows_dev, col_first, cols_dev)[:, :, None]
    sig_left = jax.nn.sigmoid(part_one)
    sig_right = jax.nn.sigmoid(part_three)
    left = (mask * sig_left * part_zero).astype(jnp.bfloat16)
    right = (mask * sig_right * part_two).astype(jnp.bfloat16)
    right_all = lax.all_gather(right, "row", axis=0, tiled=True)
    piece = right_all
    tri_turned = lax.psum_scatter(
        jnp.einsum("jkc,ikc->jic", piece, left, preferred_element_type=jnp.float32).astype(
            jnp.bfloat16
        ),
        "col",
        scatter_dimension=0,
        tiled=True,
    ).astype(jnp.float32)
    tri = jnp.transpose(tri_turned, (1, 0, 2))
    tnorm, tri_hat, tri_inverse = layer_norm(tri, gain_out)
    tnorm_low = tnorm.astype(jnp.bfloat16)
    gate = jax.nn.sigmoid(jnp.dot(normed_low, w_gate, preferred_element_type=jnp.float32))
    proj_out = jnp.dot(tnorm_low, w_out, preferred_element_type=jnp.float32)
    upstream = grad_out.astype(jnp.float32)
    d_out = (upstream * gate).astype(jnp.bfloat16)
    d_gate = upstream * proj_out * gate * (1.0 - gate)
    d_tnorm = jnp.dot(d_out, w_out.T, preferred_element_type=jnp.float32)
    d_tri = norm_back(d_tnorm, gain_out, tri_hat, tri_inverse).astype(jnp.bfloat16)
    d_tri_all = lax.all_gather(d_tri, "col", axis=1, tiled=True)
    d_left = jnp.einsum("ijc,jkc->ikc", d_tri_all, right_all, preferred_element_type=jnp.float32)
    piece = d_tri_all
    d_right = lax.psum_scatter(
        jnp.einsum("ijc,ikc->jkc", piece, left, preferred_element_type=jnp.float32).astype(
            jnp.bfloat16
        ),
        "row",
        scatter_dimension=0,
        tiled=True,
    ).astype(jnp.float32)
    d_zero = d_left * mask * sig_left
    d_one = d_left * mask * part_zero * sig_left * (1.0 - sig_left)
    d_two = d_right * mask * sig_right
    d_three = d_right * mask * part_two * sig_right * (1.0 - sig_right)
    d_all = jnp.concatenate([d_zero, d_one, d_two, d_three, d_gate], axis=-1).astype(jnp.bfloat16)
    w_back = jnp.concatenate([w_proj, w_gate], axis=1)
    d_normed = jnp.dot(d_all, w_back.T, preferred_element_type=jnp.float32)
    return norm_back(d_normed, gain_in, scaled, inverse).astype(jnp.bfloat16)


MESH = pl.DeviceIdType.MESH
STEP_ROWS = 16
NT = (((1,), (1,)), ((), ()))
TN = (((0,), (0,)), ((), ()))


def dot(left, right, dims=(((1,), (0,)), ((), ()))):
    return lax.dot_general(left, right, dims, preferred_element_type=jnp.float32)


def swap_groups(tiles, group):
    count = len(tiles)
    lane = lax.broadcasted_iota(jnp.int32, tiles[0].shape, 1)
    width = tiles[0].shape[1]
    tiles = list(tiles)
    bit = 1
    while bit < count:
        shift = bit * group
        high = (lane // shift) % 2 == 1
        for low_at in range(count):
            if low_at & bit:
                continue
            low, top = tiles[low_at], tiles[low_at | bit]
            if 2 * shift == width:
                moved = pltpu.roll(jnp.where(high, low, top), shift, 1)
                tiles[low_at] = jnp.where(high, moved, low)
                tiles[low_at | bit] = jnp.where(high, top, moved)
            else:
                tiles[low_at] = jnp.where(high, pltpu.roll(top, shift, 1), low)
                tiles[low_at | bit] = jnp.where(high, top, pltpu.roll(low, width - shift, 1))
        bit *= 2
    return tiles


def kernel(
    sizes, keep_ref, pair_hbm, up_hbm, w_proj_hbm, w_gate_hbm, w_out_hbm, gain_in_hbm, gain_out_hbm,
    out_ref,
    pair_ref, up_ref, w_proj_ref, w_gate_ref, w_out_ref, gain_in_ref, gain_out_ref,
    normed_s, pz_s, so_s, pt_s, st_s, dg_s, gq_s, tn_s, total_s, flip_a,
    send_r, send_l, recv_r, recv_l, recv_x, rp_s, xp_s, tri_s, recv_t, send_dt, recv_dt,
    send_dx, recv_dx, dl_s, dr_s, recv_dl, recv_dr,
    in_sem, send_sem, recv_sem, cross_sem, far_sem,
):
    n_row, n_col, rows, cols, chans, group = sizes
    half_rows, half_cols = n_row // 2, n_col // 2
    n_dev = half_rows * n_col
    wide_lanes = cols * group
    height = half_rows * rows
    lanes = n_col * wide_lanes
    half_lanes = lanes // 2
    step_pos = STEP_ROWS * cols
    n_step = rows // STEP_ROWS
    half_count = rows // 2
    my_row, my_col = lax.axis_index("row"), lax.axis_index("col")
    half = my_row // half_rows
    local_row = my_row % half_rows
    me = local_row * n_col + my_col
    across = ((my_row + half_rows) % n_row, my_col)

    loads = [
        pltpu.make_async_copy(src, dst, in_sem.at[at])
        for at, (src, dst) in enumerate(
            [
                (pair_hbm, pair_ref), (w_proj_hbm, w_proj_ref), (gain_in_hbm, gain_in_ref),
                (up_hbm, up_ref), (w_gate_hbm, w_gate_ref), (w_out_hbm, w_out_ref),
                (gain_out_hbm, gain_out_ref),
            ]
        )
    ]
    for load in loads:
        load.start()

    def place(local):
        return half * half_rows + local // n_col, local % n_col

    barrier = pltpu.get_barrier_semaphore()

    def greet(step, carry):
        pl.semaphore_signal(
            barrier, inc=1, device_id=place((me + step) % n_dev), device_id_type=MESH
        )
        return carry

    lax.fori_loop(1, n_dev, greet, 0)
    pl.semaphore_signal(barrier, inc=1, device_id=across, device_id_type=MESH)

    def wide(ref, local, part, mixed):
        row_at, col_at = local // n_col, local % n_col
        first = row_at * rows + part * half_count
        if mixed:
            first = (part * half_rows + row_at) * half_count
        return ref.at[
            pl.ds(pl.multiple_of(first, half_count), half_count),
            pl.ds(pl.multiple_of(col_at * wide_lanes, wide_lanes), wide_lanes),
        ]

    def tile(ref, local, part):
        return ref.at[local, part * half_count : (part + 1) * half_count]

    def remote(phase, src, dst, other):
        return pltpu.make_async_remote_copy(
            src_ref=src, dst_ref=dst, send_sem=send_sem.at[phase, other],
            recv_sem=recv_sem.at[phase], device_id=place(other), device_id_type=MESH)

    class ToWide:
        def __init__(self, phase, src, dst, part, mixed):
            self.phase, self.src, self.dst, self.part = phase, src, dst, part
            self.mixed = mixed

        def views(self, other):
            return tile(self.src, other, self.part), wide(self.dst, me, self.part, self.mixed)

        def copy(self, other):
            return remote(self.phase, *self.views(other), other)

        def own(self):
            return pltpu.make_async_copy(*self.views(me), recv_sem.at[self.phase])

        def send(self, other):
            @pl.when(other != me)
            def _():
                self.copy(other).start()

            @pl.when(other == me)
            def _():
                self.own().start()

    class FromWide(ToWide):
        def views(self, other):
            return wide(self.src, other, self.part, self.mixed), tile(self.dst, me, self.part)

    def start(exchange):
        def one(step, carry):
            exchange.copy((me + step) % n_dev).start()
            return carry

        lax.fori_loop(1, n_dev, one, 0)
        exchange.own().start()

    def start_row(exchange, row):
        for step in range(n_col):
            exchange.send(row * n_col + (my_col + step) % n_col)

    def start_col(exchange, col):
        for step in range(half_rows):
            exchange.send(((local_row + step) % half_rows) * n_col + col)

    def arrived(phase, dst):
        pltpu.make_async_copy(dst, dst, recv_sem.at[phase]).wait()

    def sent(exchange):
        def one(step, carry):
            exchange.copy((me + step) % n_dev).wait_send()
            return carry

        lax.fori_loop(1, n_dev, one, 0)

    def cross(kind, at, src, dst):
        return pltpu.make_async_remote_copy(
            src_ref=src, dst_ref=dst, send_sem=cross_sem.at[2 * kind, at],
            recv_sem=cross_sem.at[2 * kind + 1, at], device_id=across, device_id_type=MESH)

    def chunk(at):
        return pl.ds(pl.multiple_of(at * step_pos, step_pos), step_pos)

    def chunk_rows(at):
        return pl.ds(pl.multiple_of(at * STEP_ROWS, STEP_ROWS), STEP_ROWS)

    def scatter_lanes(values, dst, at):
        flip_a[...] = values
        for part in range(cols // n_dev):
            tiles = [
                flip_a[pl.ds(part * n_dev + k, STEP_ROWS, stride=cols), :] for k in range(n_dev)
            ]
            for dev, tile in enumerate(swap_groups(tiles, group)):
                dst[dev, chunk_rows(at), part * chans : (part + 1) * chans] = tile.astype(
                    jnp.bfloat16
                )

    def gather_lanes(src, at, other=None):
        for part in range(cols // n_dev):
            tiles = [
                src[dev, chunk_rows(at), part * chans : (part + 1) * chans].astype(jnp.float32)
                for dev in range(n_dev)
            ]
            if other is not None:
                tiles = [
                    tile
                    + other[dev, chunk_rows(at), part * chans : (part + 1) * chans].astype(
                        jnp.float32
                    )
                    for dev, tile in enumerate(tiles)
                ]
            for k, tile in enumerate(swap_groups(tiles, group)):
                flip_a[pl.ds(part * n_dev + k, STEP_ROWS, stride=cols), :] = tile
        return flip_a[...]

    for load in loads[:3]:
        load.wait()
    gain_in = gain_in_ref[...]
    mask = keep_ref[(my_row * rows) // BS, (my_col * cols) // BS].astype(jnp.float32)

    def project_right(at, carry):
        values = pair_ref[chunk_rows(at)].reshape(step_pos, chans).astype(jnp.float32)
        normed, _, _ = layer_norm(values, gain_in)
        low = normed.astype(jnp.bfloat16)
        normed_s[chunk(at)] = low
        value = dot(low, w_proj_ref[:, 2 * chans : 3 * chans])
        sig = jax.nn.sigmoid(dot(low, w_proj_ref[:, 3 * chans : 4 * chans]))
        pt_s[chunk(at)] = value
        st_s[chunk(at)] = sig
        scatter_lanes(mask * sig * value, send_r, at)
        return carry

    def project_left(at, carry):
        low = normed_s[chunk(at)]
        value = dot(low, w_proj_ref[:, 0:chans])
        sig = jax.nn.sigmoid(dot(low, w_proj_ref[:, chans : 2 * chans]))
        pz_s[chunk(at)] = value
        so_s[chunk(at)] = sig
        scatter_lanes(mask * sig * value, send_l, at)
        return carry

    steps = [(part * n_step // 2, (part + 1) * n_step // 2) for part in range(2)]
    ex_r = [ToWide(part, send_r, recv_r, part, False) for part in range(2)]
    ex_l = [ToWide(2 + part, send_l, recv_l, part, True) for part in range(2)]
    ex_t = [FromWide(4 + part, tri_s, recv_t, part, True) for part in range(2)]
    ex_dt = [ToWide(6 + part, send_dt, recv_dt, part, True) for part in range(2)]
    ex_dl = [FromWide(8 + part, dl_s, recv_dl, part, True) for part in range(2)]
    ex_dr = [FromWide(10 + part, dr_s, recv_dr, part, False) for part in range(2)]
    lax.fori_loop(*steps[0], project_right, 0)
    pl.semaphore_wait(barrier, n_dev)
    start(ex_r[0])
    lax.fori_loop(*steps[1], project_right, 0)
    start(ex_r[1])
    for part in range(2):
        lax.fori_loop(*steps[part], project_left, 0)
        start(ex_l[part])

    for load in loads[3:]:
        load.wait()

    @pl.when(my_col < half_cols)
    def _():
        def clear(at, carry):
            recv_dx[at] = jnp.zeros((rows, wide_lanes), jnp.bfloat16)
            return carry

        lax.fori_loop(0, n_dev, clear, 0)

    gain_out = gain_out_ref[...]

    def upstream_part(at, carry):
        gate = jax.nn.sigmoid(dot(normed_s[chunk(at)], w_gate_ref[...]))
        up = up_ref[chunk_rows(at)].reshape(step_pos, chans).astype(jnp.float32)
        weighted = up * gate
        dg_s[chunk(at)] = weighted * (1.0 - gate)
        gq_s[chunk(at)] = dot(weighted.astype(jnp.bfloat16), w_out_ref[...], NT)
        return carry

    block_j = cols
    block = block_j * group
    n_block = height // block_j
    row_id = lax.broadcasted_iota(jnp.int32, (block, block_j), 0)
    col_id = lax.broadcasted_iota(jnp.int32, (block, block_j), 1)
    spread = (row_id // group == col_id).astype(jnp.float32).astype(jnp.bfloat16)

    def same(count):
        return (
            lax.broadcasted_iota(jnp.int32, (block, count), 0) % group
            == lax.broadcasted_iota(jnp.int32, (block, count), 1) % group
        )

    def block_rows(at):
        return pl.ds(pl.multiple_of(at * block, block), block)

    def j_rows(at):
        return pl.ds(pl.multiple_of(at * block_j, block_j), block_j)

    def own_lanes(at):
        return pl.ds(pl.multiple_of(half * half_lanes + at * block, block), block)

    def far_lanes(at):
        return pl.ds(pl.multiple_of((1 - half) * half_lanes + at * block, block), block)

    late = slice(half_lanes, lanes)
    per_tile = rows // block_j
    halves = [
        [tile_at * per_tile + part * (per_tile // 2) + extra
         for tile_at in range(half_rows) for extra in range(per_tile // 2)]
        for part in range(2)
    ]
    cross_x = [
        cross(0, at, recv_r.at[j_rows(at), late], recv_x.at[j_rows(at), :])
        for at in range(n_block)
    ]
    half_view = slice(0, height // 2)
    half_tiles = slice(0, n_dev // 2)
    mid = height // 2
    for part in range(2):
        arrived(part, recv_r.at[half_view])
        for at in halves[part]:
            cross_x[at].start()

    def widen(at, carry):
        wide_rows = dot(spread, recv_r[j_rows(at), :])
        rp_s[block_rows(at), :] = jnp.where(same(lanes), wide_rows, 0.0).astype(jnp.bfloat16)
        return carry

    lax.fori_loop(0, n_block, widen, 0)
    lax.fori_loop(0, n_step, upstream_part, 0)

    def near_triangle(part, step, carry):
        at = (step + my_col) % n_block
        rows_at = slice(part * mid, (part + 1) * mid)
        tri_s[rows_at, own_lanes(at)] = dot(
            recv_l[rows_at, :], rp_s[block_rows(at), :], NT
        ).astype(jnp.bfloat16)
        start_col(ex_t[part], half * half_cols + at)
        return carry

    def widen_far(at, carry):
        wide_rows = dot(spread, recv_x[j_rows(at), :])
        xp_s[block_rows(at), :] = jnp.where(same(half_lanes), wide_rows, 0.0).astype(jnp.bfloat16)
        return carry

    def far_triangle(part, step, carry):
        at = (step + my_col) % n_block
        rows_at = slice(part * mid, (part + 1) * mid)
        tri_s[rows_at, far_lanes(at)] = dot(
            recv_l[rows_at, late], xp_s[block_rows(at), :], NT
        ).astype(jnp.bfloat16)
        start_col(ex_t[part], (1 - half) * half_cols + at)
        return carry

    for part in range(2):
        arrived(2 + part, recv_l.at[half_view])
        lax.fori_loop(0, n_block, functools.partial(near_triangle, part), 0)
        if part == 0:
            for copy in cross_x:
                copy.wait_recv()
            lax.fori_loop(0, n_block, widen_far, 0)
        lax.fori_loop(0, n_block, functools.partial(far_triangle, part), 0)

    def norm_part(at, carry):
        tri = gather_lanes(recv_t, at)
        tnorm, tri_hat, tri_inverse = layer_norm(tri, gain_out)
        tn_s[chunk(at)] = tnorm.astype(jnp.bfloat16)
        d_tri = norm_back(gq_s[chunk(at)], gain_out, tri_hat, tri_inverse)
        scatter_lanes(d_tri, send_dt, at)
        return carry

    for part in range(2):
        arrived(4 + part, recv_t.at[half_tiles])
        lax.fori_loop(*steps[part], norm_part, 0)
        start(ex_dt[part])

    def gate_part(at, carry):
        d_gate = dg_s[chunk(at)] * dot(tn_s[chunk(at)], w_out_ref[...])
        total_s[chunk(at)] = dot(d_gate.astype(jnp.bfloat16), w_gate_ref[...], NT)
        return carry

    def norm_again(at, carry):
        values = pair_ref[chunk_rows(at)].reshape(step_pos, chans).astype(jnp.float32)
        _, scaled, inverse = layer_norm(values, gain_in)
        gq_s[chunk(at)] = scaled
        dg_s[chunk(at)] = jnp.broadcast_to(inverse, scaled.shape)
        return carry

    lax.fori_loop(0, n_step, gate_part, 0)
    lax.fori_loop(0, n_step, norm_again, 0)
    for exchange in (*ex_r, *ex_l):
        sent(exchange)
    for copy in cross_x:
        copy.wait_send()

    def far_right_grad(at, carry):
        full = dot(recv_dt[:, far_lanes(at)], recv_l[:, late], TN)
        full = jnp.where(same(half_lanes), full, 0.0).astype(jnp.bfloat16)
        send_dx[j_rows(at), :] = dot(spread, full, TN).astype(jnp.bfloat16)
        return carry

    def far_copy(at, col, part):
        lanes_at = slice(col * wide_lanes, (col + 1) * wide_lanes)
        return pltpu.make_async_remote_copy(
            src_ref=send_dx.at[j_rows(at), lanes_at],
            dst_ref=recv_dx.at[me, part * half_count : (part + 1) * half_count],
            send_sem=far_sem.at[at, col], recv_sem=recv_sem.at[12 + part],
            device_id=((1 - half) * half_rows + at // per_tile, half_cols + col),
            device_id_type=MESH)

    def left_grad(part, step, carry):
        at = (step + my_col) % n_block
        rows_at = slice(part * mid, (part + 1) * mid)
        early = block_rows(at)
        near = recv_dt[rows_at, pl.ds(pl.multiple_of(half * half_lanes, half_lanes), half_lanes)]
        far = recv_dt[
            rows_at, pl.ds(pl.multiple_of((1 - half) * half_lanes, half_lanes), half_lanes)
        ]
        dl_s[rows_at, early] = dot(near, rp_s[:, early]).astype(jnp.bfloat16)
        tail = pl.ds(pl.multiple_of(half_lanes + at * block, block), block)
        dl_s[rows_at, tail] = (dot(near, rp_s[:, tail]) + dot(far, xp_s[:, early])).astype(
            jnp.bfloat16
        )
        start_col(ex_dl[part], at)
        start_col(ex_dl[part], half_cols + at)
        return carry

    def near_right_grad(at, carry):
        full = dot(recv_dt[:, own_lanes(at)], recv_l[...], TN)
        full = jnp.where(same(lanes), full, 0.0).astype(jnp.bfloat16)
        dr_s[j_rows(at), :] = dot(spread, full, TN).astype(jnp.bfloat16)
        return carry

    arrived(6, recv_dt.at[half_view])
    lax.fori_loop(0, n_block, functools.partial(left_grad, 0), 0)
    arrived(7, recv_dt.at[half_view])

    def far_step(part, step, carry):
        at = step * per_tile + part
        far_right_grad(at, 0)
        for col in range(half_cols):
            far_copy(at, col, part).start()
        return carry

    def near_step(part, step, carry):
        near_right_grad(step * per_tile + part, 0)
        start_row(ex_dr[part], step)
        return carry

    lax.fori_loop(0, half_rows, functools.partial(far_step, 0), 0)
    lax.fori_loop(0, half_rows, functools.partial(far_step, 1), 0)
    lax.fori_loop(0, n_block, functools.partial(left_grad, 1), 0)
    lax.fori_loop(0, half_rows, functools.partial(near_step, 0), 0)
    lax.fori_loop(0, half_rows, functools.partial(near_step, 1), 0)

    def finish_left(at, carry):
        d_left = gather_lanes(recv_dl, at) * mask
        sig = so_s[chunk(at)]
        d_zero = d_left * sig
        d_one = d_zero * pz_s[chunk(at)] * (1.0 - sig)
        total = total_s[chunk(at)]
        total = total + dot(d_zero.astype(jnp.bfloat16), w_proj_ref[:, 0:chans], NT)
        total = total + dot(d_one.astype(jnp.bfloat16), w_proj_ref[:, chans : 2 * chans], NT)
        total_s[chunk(at)] = total
        return carry

    for part in range(2):
        arrived(8 + part, recv_dl.at[half_tiles])
        lax.fori_loop(*steps[part], finish_left, 0)
    for exchange in (*ex_t, *ex_dt, *ex_dl):
        sent(exchange)

    def far_sent(at, carry):
        for col in range(half_cols):
            far_copy(at, col, 0).wait_send()
        return carry

    lax.fori_loop(0, n_block, far_sent, 0)

    def finish_right(at, carry):
        total = total_s[chunk(at)]
        d_right = gather_lanes(recv_dr, at, recv_dx) * mask
        sig = st_s[chunk(at)]
        d_two = d_right * sig
        d_three = d_two * pt_s[chunk(at)] * (1.0 - sig)
        total = total + dot(d_two.astype(jnp.bfloat16), w_proj_ref[:, 2 * chans : 3 * chans], NT)
        total = total + dot(d_three.astype(jnp.bfloat16), w_proj_ref[:, 3 * chans : 4 * chans], NT)
        scaled, inverse = gq_s[chunk(at)], dg_s[chunk(at)]
        result = norm_back(total, gain_in, scaled, inverse).astype(jnp.bfloat16)
        out_ref[chunk_rows(at)] = result.reshape(STEP_ROWS, cols, chans)
        return carry

    for part in range(2):
        arrived(10 + part, recv_dr.at[half_tiles])

        @pl.when(my_col >= half_cols)
        def _():
            arrived(12 + part, recv_dx.at[half_tiles])

        lax.fori_loop(*steps[part], finish_right, 0)
    for exchange in ex_dr:
        sent(exchange)


def spread_channels(sizes, pair, grad_out, keep, w_proj, w_gate, w_out, gain_in, gain_out):
    n_row, n_col, rows, cols, chans, group = sizes
    n_dev = n_row // 2 * n_col
    pos = rows * cols
    step_pos = STEP_ROWS * cols
    wide_lanes = cols * group
    height, lanes = n_row // 2 * rows, n_col * wide_lanes
    low, full = jnp.bfloat16, jnp.float32
    vmem = pl.BlockSpec(memory_space=pltpu.VMEM)
    hbm = pl.BlockSpec(memory_space=pltpu.HBM)
    flat_low = pltpu.VMEM((pos, chans), low)
    flat = pltpu.VMEM((pos, chans), full)
    tiles = pltpu.VMEM((n_dev, rows, wide_lanes), low)
    whole = pltpu.VMEM((height, lanes), low)
    part = pltpu.VMEM((height, lanes // 2), low)
    operands = (
        pair, grad_out, w_proj, w_gate, w_out, gain_in.reshape(1, chans), gain_out.reshape(1, chans)
    )
    return pl.pallas_call(
        functools.partial(kernel, sizes),
        out_shape=jax.ShapeDtypeStruct(pair.shape, low),
        in_specs=[pl.BlockSpec(memory_space=pltpu.SMEM)] + [hbm] * 7,
        out_specs=vmem,
        scratch_shapes=[pltpu.VMEM(item.shape, item.dtype) for item in operands]
        + [
            flat_low, flat, flat, flat, flat, flat, flat, flat_low, flat,
            pltpu.VMEM((step_pos, chans), full),
            tiles, tiles, whole, whole, part,
            pltpu.VMEM((height * group, lanes), low),
            pltpu.VMEM((height * group, lanes // 2), low),
            whole, tiles, tiles, whole, part, tiles, whole, whole, tiles, tiles,
            pltpu.SemaphoreType.DMA((7,)),
            pltpu.SemaphoreType.DMA((12, n_dev)),
            pltpu.SemaphoreType.DMA((14,)),
            pltpu.SemaphoreType.DMA((2, height // cols)),
            pltpu.SemaphoreType.DMA((height // cols, n_col // 2)),
        ],
        compiler_params=pltpu.CompilerParams(
            collective_id=0, has_side_effects=True, vmem_limit_bytes=56 * 2**20
        ),
    )(keep, *operands)


def tile_body(n_row, n_col, pair, grad_out, keep, *rest):
    rows, cols, chans = pair.shape
    n_dev = n_row // 2 * n_col
    group = chans // n_dev
    fits = (
        keep.shape[0] == 2
        and n_row % 2 == 0
        and n_col % 2 == 0
        and n_row * rows == 2 * BS
        and n_col * cols == 2 * BS
        and group * n_dev == chans
        and cols % n_dev == 0
        and rows == 2 * cols
        and rows % (2 * STEP_ROWS) == 0
    )
    if fits:
        sizes = (n_row, n_col, rows, cols, chans, group)
        return spread_channels(sizes, pair, grad_out, keep, *rest)
    return on_device(pair, grad_out, keep, *rest)


def solution(mesh):
    return jax.shard_map(
        functools.partial(tile_body, mesh.shape["row"], mesh.shape["col"]),
        mesh=mesh,
        in_specs=(P("row", "col", None), P("row", "col", None), P(), P(), P(), P(), P(), P()),
        out_specs=P("row", "col", None),
        check_vma=False,
    )
```

```python
import functools

import jax
import jax.numpy as jnp
from jax import lax
from jax.experimental import pallas as pl
from jax.experimental.pallas import tpu as pltpu
from jax.sharding import PartitionSpec as P

BS = 128


def layer_norm(values, gain):
    means = jnp.mean(values, -1, keepdims=True)
    centred = values - means
    inverse = lax.rsqrt(jnp.mean(centred * centred, -1, keepdims=True) + 1e-05)
    scaled = centred * inverse
    return (scaled * gain, scaled, inverse)


def norm_back(upstream, gain, scaled, inverse):
    weighted = upstream * gain
    mean_one = jnp.mean(weighted, -1, keepdims=True)
    mean_two = jnp.mean(weighted * scaled, -1, keepdims=True)
    return inverse * (weighted - mean_one - scaled * mean_two)


def block_mask(keep, row_start, row_count, col_start, col_count):
    block_ids = jnp.arange(keep.shape[0], dtype=jnp.int32)
    row_blocks = (row_start + jnp.arange(row_count, dtype=jnp.int32)) // BS
    col_blocks = (col_start + jnp.arange(col_count, dtype=jnp.int32)) // BS
    row_pick = (row_blocks[:, None] == block_ids[None, :]).astype(jnp.float32)
    col_pick = (col_blocks[:, None] == block_ids[None, :]).astype(jnp.float32)
    picked = jnp.dot(row_pick, keep.astype(jnp.float32))
    return jnp.dot(picked, col_pick.T)


def on_device(pair, grad_out, keep, w_proj, w_gate, w_out, gain_in, gain_out):
    rows_dev, cols_dev, chans = pair.shape
    normed, scaled, inverse = layer_norm(pair.astype(jnp.float32), gain_in)
    normed_low = normed.astype(jnp.bfloat16)
    proj = jnp.dot(normed_low, w_proj, preferred_element_type=jnp.float32)
    part_zero, part_one, part_two, part_three = jnp.split(proj, 4, axis=-1)
    row_first = lax.axis_index("row") * rows_dev
    col_first = lax.axis_index("col") * cols_dev
    mask = block_mask(keep, row_first, rows_dev, col_first, cols_dev)[:, :, None]
    sig_left = jax.nn.sigmoid(part_one)
    sig_right = jax.nn.sigmoid(part_three)
    left = (mask * sig_left * part_zero).astype(jnp.bfloat16)
    right = (mask * sig_right * part_two).astype(jnp.bfloat16)
    right_all = lax.all_gather(right, "row", axis=0, tiled=True)
    piece = right_all
    tri_turned = lax.psum_scatter(
        jnp.einsum("jkc,ikc->jic", piece, left, preferred_element_type=jnp.float32).astype(
            jnp.bfloat16
        ),
        "col",
        scatter_dimension=0,
        tiled=True,
    ).astype(jnp.float32)
    tri = jnp.transpose(tri_turned, (1, 0, 2))
    tnorm, tri_hat, tri_inverse = layer_norm(tri, gain_out)
    tnorm_low = tnorm.astype(jnp.bfloat16)
    gate = jax.nn.sigmoid(jnp.dot(normed_low, w_gate, preferred_element_type=jnp.float32))
    proj_out = jnp.dot(tnorm_low, w_out, preferred_element_type=jnp.float32)
    upstream = grad_out.astype(jnp.float32)
    d_out = (upstream * gate).astype(jnp.bfloat16)
    d_gate = upstream * proj_out * gate * (1.0 - gate)
    d_tnorm = jnp.dot(d_out, w_out.T, preferred_element_type=jnp.float32)
    d_tri = norm_back(d_tnorm, gain_out, tri_hat, tri_inverse).astype(jnp.bfloat16)
    d_tri_all = lax.all_gather(d_tri, "col", axis=1, tiled=True)
    d_left = jnp.einsum("ijc,jkc->ikc", d_tri_all, right_all, preferred_element_type=jnp.float32)
    piece = d_tri_all
    d_right = lax.psum_scatter(
        jnp.einsum("ijc,ikc->jkc", piece, left, preferred_element_type=jnp.float32).astype(
            jnp.bfloat16
        ),
        "row",
        scatter_dimension=0,
        tiled=True,
    ).astype(jnp.float32)
    d_zero = d_left * mask * sig_left
    d_one = d_left * mask * part_zero * sig_left * (1.0 - sig_left)
    d_two = d_right * mask * sig_right
    d_three = d_right * mask * part_two * sig_right * (1.0 - sig_right)
    d_all = jnp.concatenate([d_zero, d_one, d_two, d_three, d_gate], axis=-1).astype(jnp.bfloat16)
    w_back = jnp.concatenate([w_proj, w_gate], axis=1)
    d_normed = jnp.dot(d_all, w_back.T, preferred_element_type=jnp.float32)
    return norm_back(d_normed, gain_in, scaled, inverse).astype(jnp.bfloat16)


MESH = pl.DeviceIdType.MESH
STEP_ROWS = 16
NT = (((1,), (1,)), ((), ()))
TN = (((0,), (0,)), ((), ()))


def dot(left, right, dims=(((1,), (0,)), ((), ()))):
    return lax.dot_general(left, right, dims, preferred_element_type=jnp.float32)


def swap_groups(tiles, group):
    count = len(tiles)
    lane = lax.broadcasted_iota(jnp.int32, tiles[0].shape, 1)
    width = tiles[0].shape[1]
    tiles = list(tiles)
    bit = 1
    while bit < count:
        shift = bit * group
        high = (lane // shift) % 2 == 1
        for low_at in range(count):
            if low_at & bit:
                continue
            low, top = tiles[low_at], tiles[low_at | bit]
            if 2 * shift == width:
                moved = pltpu.roll(jnp.where(high, low, top), shift, 1)
                tiles[low_at] = jnp.where(high, moved, low)
                tiles[low_at | bit] = jnp.where(high, top, moved)
            else:
                tiles[low_at] = jnp.where(high, pltpu.roll(top, shift, 1), low)
                tiles[low_at | bit] = jnp.where(high, top, pltpu.roll(low, width - shift, 1))
        bit *= 2
    return tiles


def kernel(
    sizes, keep_ref, pair_hbm, up_hbm, w_proj_hbm, w_gate_hbm, w_out_hbm, gain_in_hbm, gain_out_hbm,
    out_ref,
    pair_ref, up_ref, w_proj_ref, w_gate_ref, w_out_ref, gain_in_ref, gain_out_ref,
    normed_s, pz_s, so_s, pt_s, st_s, dg_s, gq_s, tn_s, total_s, flip_a,
    send_r, send_l, recv_r, recv_l, recv_x, rp_s, xp_s, tri_s, recv_t, send_dt, recv_dt,
    send_dx, recv_dx, dl_s, dr_s, recv_dl, recv_dr,
    in_sem, send_sem, recv_sem, cross_sem, far_sem, out_sem,
):
    n_row, n_col, rows, cols, chans, group = sizes
    half_rows, half_cols = n_row // 2, n_col // 2
    n_dev = half_rows * n_col
    wide_lanes = cols * group
    height = half_rows * rows
    lanes = n_col * wide_lanes
    half_lanes = lanes // 2
    step_pos = STEP_ROWS * cols
    n_step = rows // STEP_ROWS
    half_count = rows // 2
    my_row, my_col = lax.axis_index("row"), lax.axis_index("col")
    half = my_row // half_rows
    local_row = my_row % half_rows
    me = local_row * n_col + my_col
    across = ((my_row + half_rows) % n_row, my_col)

    loads = [
        pltpu.make_async_copy(src, dst, in_sem.at[at])
        for at, (src, dst) in enumerate(
            [
                (pair_hbm, pair_ref), (w_proj_hbm, w_proj_ref), (gain_in_hbm, gain_in_ref),
                (up_hbm, up_ref), (w_gate_hbm, w_gate_ref), (w_out_hbm, w_out_ref),
                (gain_out_hbm, gain_out_ref),
            ]
        )
    ]
    for load in loads:
        load.start()

    def place(local):
        return half * half_rows + local // n_col, local % n_col

    barrier = pltpu.get_barrier_semaphore()

    def greet(step, carry):
        pl.semaphore_signal(
            barrier, inc=1, device_id=place((me + step) % n_dev), device_id_type=MESH
        )
        return carry

    lax.fori_loop(1, n_dev, greet, 0)
    pl.semaphore_signal(barrier, inc=1, device_id=across, device_id_type=MESH)

    def wide(ref, local, part, mixed):
        row_at, col_at = local // n_col, local % n_col
        first = row_at * rows + part * half_count
        if mixed:
            first = (part * half_rows + row_at) * half_count
        return ref.at[
            pl.ds(pl.multiple_of(first, half_count), half_count),
            pl.ds(pl.multiple_of(col_at * wide_lanes, wide_lanes), wide_lanes),
        ]

    def tile(ref, local, part):
        return ref.at[local, part * half_count : (part + 1) * half_count]

    def remote(phase, src, dst, other):
        return pltpu.make_async_remote_copy(
            src_ref=src, dst_ref=dst, send_sem=send_sem.at[phase, other],
            recv_sem=recv_sem.at[phase], device_id=place(other), device_id_type=MESH)

    class ToWide:
        def __init__(self, phase, src, dst, part, mixed):
            self.phase, self.src, self.dst, self.part = phase, src, dst, part
            self.mixed = mixed

        def views(self, other):
            return tile(self.src, other, self.part), wide(self.dst, me, self.part, self.mixed)

        def copy(self, other):
            return remote(self.phase, *self.views(other), other)

        def own(self):
            return pltpu.make_async_copy(*self.views(me), recv_sem.at[self.phase])

        def send(self, other):
            @pl.when(other != me)
            def _():
                self.copy(other).start()

            @pl.when(other == me)
            def _():
                self.own().start()

    class FromWide(ToWide):
        def views(self, other):
            return wide(self.src, other, self.part, self.mixed), tile(self.dst, me, self.part)

    def start(exchange):
        def one(step, carry):
            exchange.copy((me + step) % n_dev).start()
            return carry

        lax.fori_loop(1, n_dev, one, 0)
        exchange.own().start()

    def start_row(exchange, row):
        for step in range(n_col):
            exchange.send(row * n_col + (my_col + step) % n_col)

    def start_col(exchange, col):
        for step in range(half_rows):
            exchange.send(((local_row + step) % half_rows) * n_col + col)

    def arrived(phase, dst):
        pltpu.make_async_copy(dst, dst, recv_sem.at[phase]).wait()

    def sent(exchange):
        def one(step, carry):
            exchange.copy((me + step) % n_dev).wait_send()
            return carry

        lax.fori_loop(1, n_dev, one, 0)

    def cross(kind, at, src, dst):
        return pltpu.make_async_remote_copy(
            src_ref=src, dst_ref=dst, send_sem=cross_sem.at[2 * kind, at],
            recv_sem=cross_sem.at[2 * kind + 1, at], device_id=across, device_id_type=MESH)

    def chunk(at):
        return pl.ds(pl.multiple_of(at * step_pos, step_pos), step_pos)

    def chunk_rows(at):
        return pl.ds(pl.multiple_of(at * STEP_ROWS, STEP_ROWS), STEP_ROWS)

    def scatter_lanes(values, dst, at):
        flip_a[...] = values
        for part in range(cols // n_dev):
            tiles = [
                flip_a[pl.ds(part * n_dev + k, STEP_ROWS, stride=cols), :] for k in range(n_dev)
            ]
            for dev, tile in enumerate(swap_groups(tiles, group)):
                dst[dev, chunk_rows(at), part * chans : (part + 1) * chans] = tile.astype(
                    jnp.bfloat16
                )

    def gather_lanes(src, at, other=None):
        for part in range(cols // n_dev):
            tiles = [
                src[dev, chunk_rows(at), part * chans : (part + 1) * chans].astype(jnp.float32)
                for dev in range(n_dev)
            ]
            if other is not None:
                tiles = [
                    tile
                    + other[dev, chunk_rows(at), part * chans : (part + 1) * chans].astype(
                        jnp.float32
                    )
                    for dev, tile in enumerate(tiles)
                ]
            for k, tile in enumerate(swap_groups(tiles, group)):
                flip_a[pl.ds(part * n_dev + k, STEP_ROWS, stride=cols), :] = tile
        return flip_a[...]

    for load in loads[:3]:
        load.wait()
    gain_in = gain_in_ref[...]
    mask = keep_ref[(my_row * rows) // BS, (my_col * cols) // BS].astype(jnp.float32)

    def project_right(at, carry):
        values = pair_ref[chunk_rows(at)].reshape(step_pos, chans).astype(jnp.float32)
        normed, _, _ = layer_norm(values, gain_in)
        low = normed.astype(jnp.bfloat16)
        normed_s[chunk(at)] = low
        value = dot(low, w_proj_ref[:, 2 * chans : 3 * chans])
        sig = jax.nn.sigmoid(dot(low, w_proj_ref[:, 3 * chans : 4 * chans]))
        pt_s[chunk(at)] = value
        st_s[chunk(at)] = sig
        scatter_lanes(mask * sig * value, send_r, at)
        return carry

    def project_left(at, carry):
        low = normed_s[chunk(at)]
        value = dot(low, w_proj_ref[:, 0:chans])
        sig = jax.nn.sigmoid(dot(low, w_proj_ref[:, chans : 2 * chans]))
        pz_s[chunk(at)] = value
        so_s[chunk(at)] = sig
        scatter_lanes(mask * sig * value, send_l, at)
        return carry

    steps = [(part * n_step // 2, (part + 1) * n_step // 2) for part in range(2)]
    ex_r = [ToWide(part, send_r, recv_r, part, False) for part in range(2)]
    ex_l = [ToWide(2 + part, send_l, recv_l, part, True) for part in range(2)]
    ex_t = [FromWide(4 + part, tri_s, recv_t, part, True) for part in range(2)]
    ex_dt = [ToWide(6 + part, send_dt, recv_dt, part, True) for part in range(2)]
    ex_dl = [FromWide(8 + part, dl_s, recv_dl, part, True) for part in range(2)]
    ex_dr = [FromWide(10 + part, dr_s, recv_dr, part, False) for part in range(2)]
    lax.fori_loop(*steps[0], project_right, 0)
    pl.semaphore_wait(barrier, n_dev)
    start(ex_r[0])
    lax.fori_loop(*steps[1], project_right, 0)
    start(ex_r[1])
    block_j = cols
    block = block_j * group
    n_block = height // block_j

    def block_rows(at):
        return pl.ds(pl.multiple_of(at * block, block), block)

    def j_rows(at):
        return pl.ds(pl.multiple_of(at * block_j, block_j), block_j)

    late = slice(half_lanes, lanes)
    per_tile = rows // block_j
    halves = [
        [tile_at * per_tile + part * (per_tile // 2) + extra
         for tile_at in range(half_rows) for extra in range(per_tile // 2)]
        for part in range(2)
    ]
    cross_x = [
        cross(0, at, recv_r.at[j_rows(at), late], recv_x.at[j_rows(at), :])
        for at in range(n_block)
    ]
    half_view = slice(0, height // 2)
    for part in range(2):
        lax.fori_loop(*steps[part], project_left, 0)
        if part == 0:
            start(ex_l[0])
        arrived(part, recv_r.at[half_view])
        for at in halves[part]:
            cross_x[at].start()
    start(ex_l[1])

    for load in loads[3:]:
        load.wait()

    @pl.when(my_col < half_cols)
    def _():
        def clear(at, carry):
            recv_dx[at] = jnp.zeros((rows, wide_lanes), jnp.bfloat16)
            return carry

        lax.fori_loop(0, n_dev, clear, 0)

    gain_out = gain_out_ref[...]

    def upstream_part(at, carry):
        gate = jax.nn.sigmoid(dot(normed_s[chunk(at)], w_gate_ref[...]))
        up = up_ref[chunk_rows(at)].reshape(step_pos, chans).astype(jnp.float32)
        weighted = up * gate
        dg_s[chunk(at)] = weighted * (1.0 - gate)
        gq_s[chunk(at)] = dot(weighted.astype(jnp.bfloat16), w_out_ref[...], NT)
        return carry

    row_id = lax.broadcasted_iota(jnp.int32, (block, block_j), 0)
    col_id = lax.broadcasted_iota(jnp.int32, (block, block_j), 1)
    spread = (row_id // group == col_id).astype(jnp.float32).astype(jnp.bfloat16)

    def same(count):
        return (
            lax.broadcasted_iota(jnp.int32, (block, count), 0) % group
            == lax.broadcasted_iota(jnp.int32, (block, count), 1) % group
        )

    def own_lanes(at):
        return pl.ds(pl.multiple_of(half * half_lanes + at * block, block), block)

    def far_lanes(at):
        return pl.ds(pl.multiple_of((1 - half) * half_lanes + at * block, block), block)

    half_tiles = slice(0, n_dev // 2)
    mid = height // 2

    def widen(at, carry):
        wide_rows = dot(spread, recv_r[j_rows(at), :])
        rp_s[block_rows(at), :] = jnp.where(same(lanes), wide_rows, 0.0).astype(jnp.bfloat16)
        return carry

    lax.fori_loop(0, n_block, widen, 0)
    lax.fori_loop(0, n_step, upstream_part, 0)

    def near_triangle(part, step, carry):
        at = (step + my_col) % n_block
        rows_at = slice(part * mid, (part + 1) * mid)
        tri_s[rows_at, own_lanes(at)] = dot(
            recv_l[rows_at, :], rp_s[block_rows(at), :], NT
        ).astype(jnp.bfloat16)
        start_col(ex_t[part], half * half_cols + at)
        return carry

    def widen_far(at, carry):
        wide_rows = dot(spread, recv_x[j_rows(at), :])
        xp_s[block_rows(at), :] = jnp.where(same(half_lanes), wide_rows, 0.0).astype(jnp.bfloat16)
        return carry

    def far_triangle(part, step, carry):
        at = (step + my_col) % n_block
        rows_at = slice(part * mid, (part + 1) * mid)
        tri_s[rows_at, far_lanes(at)] = dot(
            recv_l[rows_at, late], xp_s[block_rows(at), :], NT
        ).astype(jnp.bfloat16)
        start_col(ex_t[part], (1 - half) * half_cols + at)
        return carry

    for part in range(2):
        arrived(2 + part, recv_l.at[half_view])
        lax.fori_loop(0, n_block, functools.partial(near_triangle, part), 0)
        if part == 0:
            for copy in cross_x:
                copy.wait_recv()
            lax.fori_loop(0, n_block, widen_far, 0)
        lax.fori_loop(0, n_block, functools.partial(far_triangle, part), 0)

    def norm_part(at, carry):
        tri = gather_lanes(recv_t, at)
        tnorm, tri_hat, tri_inverse = layer_norm(tri, gain_out)
        tn_s[chunk(at)] = tnorm.astype(jnp.bfloat16)
        d_tri = norm_back(gq_s[chunk(at)], gain_out, tri_hat, tri_inverse)
        scatter_lanes(d_tri, send_dt, at)
        return carry

    for part in range(2):
        arrived(4 + part, recv_t.at[half_tiles])
        lax.fori_loop(*steps[part], norm_part, 0)
        start(ex_dt[part])

    def gate_part(at, carry):
        d_gate = dg_s[chunk(at)] * dot(tn_s[chunk(at)], w_out_ref[...])
        total_s[chunk(at)] = dot(d_gate.astype(jnp.bfloat16), w_gate_ref[...], NT)
        return carry

    def norm_again(at, carry):
        values = pair_ref[chunk_rows(at)].reshape(step_pos, chans).astype(jnp.float32)
        _, scaled, inverse = layer_norm(values, gain_in)
        gq_s[chunk(at)] = scaled
        dg_s[chunk(at)] = jnp.broadcast_to(inverse, scaled.shape)
        return carry

    lax.fori_loop(0, n_step, gate_part, 0)
    lax.fori_loop(0, n_step, norm_again, 0)
    for exchange in (*ex_r, *ex_l):
        sent(exchange)
    for copy in cross_x:
        copy.wait_send()

    def far_right_grad(at, carry):
        full = dot(recv_dt[:, far_lanes(at)], recv_l[:, late], TN)
        full = jnp.where(same(half_lanes), full, 0.0).astype(jnp.bfloat16)
        send_dx[j_rows(at), :] = dot(spread, full, TN).astype(jnp.bfloat16)
        return carry

    def far_copy(at, col, part):
        lanes_at = slice(col * wide_lanes, (col + 1) * wide_lanes)
        return pltpu.make_async_remote_copy(
            src_ref=send_dx.at[j_rows(at), lanes_at],
            dst_ref=recv_dx.at[me, part * half_count : (part + 1) * half_count],
            send_sem=far_sem.at[at, col], recv_sem=recv_sem.at[12 + part],
            device_id=((1 - half) * half_rows + at // per_tile, half_cols + col),
            device_id_type=MESH)

    def left_grad(part, step, carry):
        at = (step + my_col) % n_block
        rows_at = slice(part * mid, (part + 1) * mid)
        early = block_rows(at)
        near = recv_dt[rows_at, pl.ds(pl.multiple_of(half * half_lanes, half_lanes), half_lanes)]
        far = recv_dt[
            rows_at, pl.ds(pl.multiple_of((1 - half) * half_lanes, half_lanes), half_lanes)
        ]
        dl_s[rows_at, early] = dot(near, rp_s[:, early]).astype(jnp.bfloat16)
        tail = pl.ds(pl.multiple_of(half_lanes + at * block, block), block)
        dl_s[rows_at, tail] = (dot(near, rp_s[:, tail]) + dot(far, xp_s[:, early])).astype(
            jnp.bfloat16
        )
        start_col(ex_dl[part], at)
        start_col(ex_dl[part], half_cols + at)
        return carry

    def near_right_grad(at, carry):
        full = dot(recv_dt[:, own_lanes(at)], recv_l[...], TN)
        full = jnp.where(same(lanes), full, 0.0).astype(jnp.bfloat16)
        dr_s[j_rows(at), :] = dot(spread, full, TN).astype(jnp.bfloat16)
        return carry

    arrived(6, recv_dt.at[half_view])
    lax.fori_loop(0, n_block, functools.partial(left_grad, 0), 0)
    arrived(7, recv_dt.at[half_view])

    def far_step(part, step, carry):
        at = step * per_tile + part
        far_right_grad(at, 0)
        for col in range(half_cols):
            far_copy(at, col, part).start()
        return carry

    def near_step(part, step, carry):
        near_right_grad(step * per_tile + part, 0)
        start_row(ex_dr[part], step)
        return carry

    lax.fori_loop(0, n_block, functools.partial(left_grad, 1), 0)
    lax.fori_loop(0, half_rows, functools.partial(far_step, 0), 0)
    lax.fori_loop(0, half_rows, functools.partial(far_step, 1), 0)
    lax.fori_loop(0, half_rows, functools.partial(near_step, 0), 0)
    lax.fori_loop(0, half_rows, functools.partial(near_step, 1), 0)

    def finish_left(at, carry):
        d_left = gather_lanes(recv_dl, at) * mask
        sig = so_s[chunk(at)]
        d_zero = d_left * sig
        d_one = d_zero * pz_s[chunk(at)] * (1.0 - sig)
        total = total_s[chunk(at)]
        total = total + dot(d_zero.astype(jnp.bfloat16), w_proj_ref[:, 0:chans], NT)
        total = total + dot(d_one.astype(jnp.bfloat16), w_proj_ref[:, chans : 2 * chans], NT)
        total_s[chunk(at)] = total
        return carry

    for part in range(2):
        arrived(8 + part, recv_dl.at[half_tiles])
        lax.fori_loop(*steps[part], finish_left, 0)
    for exchange in (*ex_t, *ex_dt, *ex_dl):
        sent(exchange)

    def far_sent(at, carry):
        for col in range(half_cols):
            far_copy(at, col, 0).wait_send()
        return carry

    lax.fori_loop(0, n_block, far_sent, 0)

    def out_copy(at):
        return pltpu.make_async_copy(
            pair_ref.at[chunk_rows(at)], out_ref.at[chunk_rows(at)], out_sem.at[at]
        )

    def finish_right(at, carry):
        total = total_s[chunk(at)]
        d_right = gather_lanes(recv_dr, at, recv_dx) * mask
        sig = st_s[chunk(at)]
        d_two = d_right * sig
        d_three = d_two * pt_s[chunk(at)] * (1.0 - sig)
        total = total + dot(d_two.astype(jnp.bfloat16), w_proj_ref[:, 2 * chans : 3 * chans], NT)
        total = total + dot(d_three.astype(jnp.bfloat16), w_proj_ref[:, 3 * chans : 4 * chans], NT)
        scaled, inverse = gq_s[chunk(at)], dg_s[chunk(at)]
        result = norm_back(total, gain_in, scaled, inverse).astype(jnp.bfloat16)
        pair_ref[chunk_rows(at)] = result.reshape(STEP_ROWS, cols, chans)
        out_copy(at).start()
        return carry

    for part in range(2):
        arrived(10 + part, recv_dr.at[half_tiles])

        @pl.when(my_col >= half_cols)
        def _():
            arrived(12 + part, recv_dx.at[half_tiles])

        lax.fori_loop(*steps[part], finish_right, 0)
    for exchange in ex_dr:
        sent(exchange)
    for at in range(n_step):
        out_copy(at).wait()


def spread_channels(sizes, pair, grad_out, keep, w_proj, w_gate, w_out, gain_in, gain_out):
    n_row, n_col, rows, cols, chans, group = sizes
    n_dev = n_row // 2 * n_col
    pos = rows * cols
    step_pos = STEP_ROWS * cols
    wide_lanes = cols * group
    height, lanes = n_row // 2 * rows, n_col * wide_lanes
    low, full = jnp.bfloat16, jnp.float32
    hbm = pl.BlockSpec(memory_space=pltpu.HBM)
    flat_low = pltpu.VMEM((pos, chans), low)
    flat = pltpu.VMEM((pos, chans), full)
    tiles = pltpu.VMEM((n_dev, rows, wide_lanes), low)
    whole = pltpu.VMEM((height, lanes), low)
    part = pltpu.VMEM((height, lanes // 2), low)
    operands = (
        pair, grad_out, w_proj, w_gate, w_out, gain_in.reshape(1, chans), gain_out.reshape(1, chans)
    )
    return pl.pallas_call(
        functools.partial(kernel, sizes),
        out_shape=jax.ShapeDtypeStruct(pair.shape, low),
        in_specs=[pl.BlockSpec(memory_space=pltpu.SMEM)] + [hbm] * 7,
        out_specs=pl.BlockSpec(memory_space=pl.ANY),
        scratch_shapes=[pltpu.VMEM(item.shape, item.dtype) for item in operands]
        + [
            flat_low, flat, flat, flat, flat, flat, flat, flat_low, flat,
            pltpu.VMEM((step_pos, chans), full),
            tiles, tiles, whole, whole, part,
            pltpu.VMEM((height * group, lanes), low),
            pltpu.VMEM((height * group, lanes // 2), low),
            whole, tiles, tiles, whole, part, tiles, whole, whole, tiles, tiles,
            pltpu.SemaphoreType.DMA((7,)),
            pltpu.SemaphoreType.DMA((12, n_dev)),
            pltpu.SemaphoreType.DMA((14,)),
            pltpu.SemaphoreType.DMA((2, height // cols)),
            pltpu.SemaphoreType.DMA((height // cols, n_col // 2)),
            pltpu.SemaphoreType.DMA((rows // STEP_ROWS,)),
        ],
        compiler_params=pltpu.CompilerParams(
            collective_id=0, has_side_effects=True, vmem_limit_bytes=56 * 2**20
        ),
    )(keep, *operands)


def tile_body(n_row, n_col, pair, grad_out, keep, *rest):
    rows, cols, chans = pair.shape
    n_dev = n_row // 2 * n_col
    group = chans // n_dev
    fits = (
        keep.shape[0] == 2
        and n_row % 2 == 0
        and n_col % 2 == 0
        and n_row * rows == 2 * BS
        and n_col * cols == 2 * BS
        and group * n_dev == chans
        and cols % n_dev == 0
        and rows == 2 * cols
        and rows % (2 * STEP_ROWS) == 0
    )
    if fits:
        sizes = (n_row, n_col, rows, cols, chans, group)
        return spread_channels(sizes, pair, grad_out, keep, *rest)
    return on_device(pair, grad_out, keep, *rest)


def solution(mesh):
    return jax.shard_map(
        functools.partial(tile_body, mesh.shape["row"], mesh.shape["col"]),
        mesh=mesh,
        in_specs=(P("row", "col", None), P("row", "col", None), P(), P(), P(), P(), P(), P()),
        out_specs=P("row", "col", None),
        check_vma=False,
    )
```

```python
import functools

import jax
import jax.numpy as jnp
from jax import lax
from jax.experimental import pallas as pl
from jax.experimental.pallas import tpu as pltpu
from jax.sharding import PartitionSpec as P

BS = 128


def layer_norm(values, gain):
    means = jnp.mean(values, -1, keepdims=True)
    centred = values - means
    inverse = lax.rsqrt(jnp.mean(centred * centred, -1, keepdims=True) + 1e-05)
    scaled = centred * inverse
    return (scaled * gain, scaled, inverse)


def norm_back(upstream, gain, scaled, inverse):
    weighted = upstream * gain
    mean_one = jnp.mean(weighted, -1, keepdims=True)
    mean_two = jnp.mean(weighted * scaled, -1, keepdims=True)
    return inverse * (weighted - mean_one - scaled * mean_two)


def block_mask(keep, row_start, row_count, col_start, col_count):
    block_ids = jnp.arange(keep.shape[0], dtype=jnp.int32)
    row_blocks = (row_start + jnp.arange(row_count, dtype=jnp.int32)) // BS
    col_blocks = (col_start + jnp.arange(col_count, dtype=jnp.int32)) // BS
    row_pick = (row_blocks[:, None] == block_ids[None, :]).astype(jnp.float32)
    col_pick = (col_blocks[:, None] == block_ids[None, :]).astype(jnp.float32)
    picked = jnp.dot(row_pick, keep.astype(jnp.float32))
    return jnp.dot(picked, col_pick.T)


def on_device(pair, grad_out, keep, w_proj, w_gate, w_out, gain_in, gain_out):
    rows_dev, cols_dev, chans = pair.shape
    normed, scaled, inverse = layer_norm(pair.astype(jnp.float32), gain_in)
    normed_low = normed.astype(jnp.bfloat16)
    proj = jnp.dot(normed_low, w_proj, preferred_element_type=jnp.float32)
    part_zero, part_one, part_two, part_three = jnp.split(proj, 4, axis=-1)
    row_first = lax.axis_index("row") * rows_dev
    col_first = lax.axis_index("col") * cols_dev
    mask = block_mask(keep, row_first, rows_dev, col_first, cols_dev)[:, :, None]
    sig_left = jax.nn.sigmoid(part_one)
    sig_right = jax.nn.sigmoid(part_three)
    left = (mask * sig_left * part_zero).astype(jnp.bfloat16)
    right = (mask * sig_right * part_two).astype(jnp.bfloat16)
    right_all = lax.all_gather(right, "row", axis=0, tiled=True)
    piece = right_all
    tri_turned = lax.psum_scatter(
        jnp.einsum("jkc,ikc->jic", piece, left, preferred_element_type=jnp.float32).astype(
            jnp.bfloat16
        ),
        "col",
        scatter_dimension=0,
        tiled=True,
    ).astype(jnp.float32)
    tri = jnp.transpose(tri_turned, (1, 0, 2))
    tnorm, tri_hat, tri_inverse = layer_norm(tri, gain_out)
    tnorm_low = tnorm.astype(jnp.bfloat16)
    gate = jax.nn.sigmoid(jnp.dot(normed_low, w_gate, preferred_element_type=jnp.float32))
    proj_out = jnp.dot(tnorm_low, w_out, preferred_element_type=jnp.float32)
    upstream = grad_out.astype(jnp.float32)
    d_out = (upstream * gate).astype(jnp.bfloat16)
    d_gate = upstream * proj_out * gate * (1.0 - gate)
    d_tnorm = jnp.dot(d_out, w_out.T, preferred_element_type=jnp.float32)
    d_tri = norm_back(d_tnorm, gain_out, tri_hat, tri_inverse).astype(jnp.bfloat16)
    d_tri_all = lax.all_gather(d_tri, "col", axis=1, tiled=True)
    d_left = jnp.einsum("ijc,jkc->ikc", d_tri_all, right_all, preferred_element_type=jnp.float32)
    piece = d_tri_all
    d_right = lax.psum_scatter(
        jnp.einsum("ijc,ikc->jkc", piece, left, preferred_element_type=jnp.float32).astype(
            jnp.bfloat16
        ),
        "row",
        scatter_dimension=0,
        tiled=True,
    ).astype(jnp.float32)
    d_zero = d_left * mask * sig_left
    d_one = d_left * mask * part_zero * sig_left * (1.0 - sig_left)
    d_two = d_right * mask * sig_right
    d_three = d_right * mask * part_two * sig_right * (1.0 - sig_right)
    d_all = jnp.concatenate([d_zero, d_one, d_two, d_three, d_gate], axis=-1).astype(jnp.bfloat16)
    w_back = jnp.concatenate([w_proj, w_gate], axis=1)
    d_normed = jnp.dot(d_all, w_back.T, preferred_element_type=jnp.float32)
    return norm_back(d_normed, gain_in, scaled, inverse).astype(jnp.bfloat16)


MESH = pl.DeviceIdType.MESH
STEP_ROWS = 16
NT = (((1,), (1,)), ((), ()))
TN = (((0,), (0,)), ((), ()))


def dot(left, right, dims=(((1,), (0,)), ((), ()))):
    return lax.dot_general(left, right, dims, preferred_element_type=jnp.float32)


def swap_groups(tiles, group):
    count = len(tiles)
    lane = lax.broadcasted_iota(jnp.int32, tiles[0].shape, 1)
    width = tiles[0].shape[1]
    tiles = list(tiles)
    bit = 1
    while bit < count:
        shift = bit * group
        high = (lane // shift) % 2 == 1
        for low_at in range(count):
            if low_at & bit:
                continue
            low, top = tiles[low_at], tiles[low_at | bit]
            if 2 * shift == width:
                moved = pltpu.roll(jnp.where(high, low, top), shift, 1)
                tiles[low_at] = jnp.where(high, moved, low)
                tiles[low_at | bit] = jnp.where(high, top, moved)
            else:
                tiles[low_at] = jnp.where(high, pltpu.roll(top, shift, 1), low)
                tiles[low_at | bit] = jnp.where(high, top, pltpu.roll(low, width - shift, 1))
        bit *= 2
    return tiles


def kernel(
    sizes, keep_ref, pair_hbm, up_hbm, w_proj_hbm, w_gate_hbm, w_out_hbm, gain_in_hbm, gain_out_hbm,
    out_ref,
    pair_ref, up_ref, w_proj_ref, w_gate_ref, w_out_ref, gain_in_ref, gain_out_ref,
    normed_s, pz_s, so_s, pt_s, st_s, dg_s, gq_s, tn_s, total_s, flip_a,
    send_r, send_l, recv_r, recv_l, recv_x, rp_s, xp_s, tri_s, recv_t, send_dt, recv_dt,
    send_dx, recv_dx, dl_s, dr_s, recv_dl, recv_dr,
    in_sem, send_sem, recv_sem, cross_sem, far_sem, out_sem,
):
    n_row, n_col, rows, cols, chans, group = sizes
    half_rows, half_cols = n_row // 2, n_col // 2
    n_dev = half_rows * n_col
    wide_lanes = cols * group
    height = half_rows * rows
    lanes = n_col * wide_lanes
    half_lanes = lanes // 2
    step_pos = STEP_ROWS * cols
    n_step = rows // STEP_ROWS
    half_count = rows // 2
    my_row, my_col = lax.axis_index("row"), lax.axis_index("col")
    half = my_row // half_rows
    local_row = my_row % half_rows
    me = local_row * n_col + my_col
    across = ((my_row + half_rows) % n_row, my_col)

    loads = [
        pltpu.make_async_copy(src, dst, in_sem.at[at])
        for at, (src, dst) in enumerate(
            [
                (pair_hbm, pair_ref), (w_proj_hbm, w_proj_ref), (gain_in_hbm, gain_in_ref),
                (up_hbm, up_ref), (w_gate_hbm, w_gate_ref), (w_out_hbm, w_out_ref),
                (gain_out_hbm, gain_out_ref),
            ]
        )
    ]
    for load in loads:
        load.start()

    def place(local):
        return half * half_rows + local // n_col, local % n_col

    barrier = pltpu.get_barrier_semaphore()

    def greet(step, carry):
        pl.semaphore_signal(
            barrier, inc=1, device_id=place((me + step) % n_dev), device_id_type=MESH
        )
        return carry

    lax.fori_loop(1, n_dev, greet, 0)
    pl.semaphore_signal(barrier, inc=1, device_id=across, device_id_type=MESH)

    def wide(ref, local, part, mixed):
        row_at, col_at = local // n_col, local % n_col
        first = row_at * rows + part * half_count
        if mixed:
            first = (part * half_rows + row_at) * half_count
        return ref.at[
            pl.ds(pl.multiple_of(first, half_count), half_count),
            pl.ds(pl.multiple_of(col_at * wide_lanes, wide_lanes), wide_lanes),
        ]

    def tile(ref, local, part):
        return ref.at[local, part * half_count : (part + 1) * half_count]

    def remote(phase, src, dst, other):
        return pltpu.make_async_remote_copy(
            src_ref=src, dst_ref=dst, send_sem=send_sem.at[phase, other],
            recv_sem=recv_sem.at[phase], device_id=place(other), device_id_type=MESH)

    class ToWide:
        def __init__(self, phase, src, dst, part, mixed):
            self.phase, self.src, self.dst, self.part = phase, src, dst, part
            self.mixed = mixed

        def views(self, other):
            return tile(self.src, other, self.part), wide(self.dst, me, self.part, self.mixed)

        def copy(self, other):
            return remote(self.phase, *self.views(other), other)

        def own(self):
            return pltpu.make_async_copy(*self.views(me), recv_sem.at[self.phase])

        def send(self, other):
            @pl.when(other != me)
            def _():
                self.copy(other).start()

            @pl.when(other == me)
            def _():
                self.own().start()

    class FromWide(ToWide):
        def views(self, other):
            return wide(self.src, other, self.part, self.mixed), tile(self.dst, me, self.part)

    def start(exchange):
        def one(step, carry):
            exchange.copy((me + step) % n_dev).start()
            return carry

        lax.fori_loop(1, n_dev, one, 0)
        exchange.own().start()

    def start_row(exchange, row):
        for step in range(n_col):
            exchange.send(row * n_col + (my_col + step) % n_col)

    def start_col(exchange, col):
        for step in range(half_rows):
            exchange.send(((local_row + step) % half_rows) * n_col + col)

    def arrived(phase, dst):
        pltpu.make_async_copy(dst, dst, recv_sem.at[phase]).wait()

    def sent(exchange):
        def one(step, carry):
            exchange.copy((me + step) % n_dev).wait_send()
            return carry

        lax.fori_loop(1, n_dev, one, 0)

    def cross(kind, at, src, dst):
        return pltpu.make_async_remote_copy(
            src_ref=src, dst_ref=dst, send_sem=cross_sem.at[2 * kind, at],
            recv_sem=cross_sem.at[2 * kind + 1, at], device_id=across, device_id_type=MESH)

    def chunk(at):
        return pl.ds(pl.multiple_of(at * step_pos, step_pos), step_pos)

    def chunk_rows(at):
        return pl.ds(pl.multiple_of(at * STEP_ROWS, STEP_ROWS), STEP_ROWS)

    def scatter_lanes(values, dst, at):
        flip_a[...] = values
        for part in range(cols // n_dev):
            tiles = [
                flip_a[pl.ds(part * n_dev + k, STEP_ROWS, stride=cols), :] for k in range(n_dev)
            ]
            for dev, tile in enumerate(swap_groups(tiles, group)):
                dst[dev, chunk_rows(at), part * chans : (part + 1) * chans] = tile.astype(
                    jnp.bfloat16
                )

    def gather_lanes(src, at, other=None):
        for part in range(cols // n_dev):
            tiles = [
                src[dev, chunk_rows(at), part * chans : (part + 1) * chans].astype(jnp.float32)
                for dev in range(n_dev)
            ]
            if other is not None:
                tiles = [
                    tile
                    + other[dev, chunk_rows(at), part * chans : (part + 1) * chans].astype(
                        jnp.float32
                    )
                    for dev, tile in enumerate(tiles)
                ]
            for k, tile in enumerate(swap_groups(tiles, group)):
                flip_a[pl.ds(part * n_dev + k, STEP_ROWS, stride=cols), :] = tile
        return flip_a[...]

    for load in loads[:3]:
        load.wait()
    gain_in = gain_in_ref[...]
    mask = keep_ref[(my_row * rows) // BS, (my_col * cols) // BS].astype(jnp.float32)

    def project_right(at, carry):
        values = pair_ref[chunk_rows(at)].reshape(step_pos, chans).astype(jnp.float32)
        normed, _, _ = layer_norm(values, gain_in)
        low = normed.astype(jnp.bfloat16)
        normed_s[chunk(at)] = low
        value = dot(low, w_proj_ref[:, 2 * chans : 3 * chans])
        sig = jax.nn.sigmoid(dot(low, w_proj_ref[:, 3 * chans : 4 * chans]))
        pt_s[chunk(at)] = value
        st_s[chunk(at)] = sig
        scatter_lanes(mask * sig * value, send_r, at)
        return carry

    def project_left(at, carry):
        low = normed_s[chunk(at)]
        value = dot(low, w_proj_ref[:, 0:chans])
        sig = jax.nn.sigmoid(dot(low, w_proj_ref[:, chans : 2 * chans]))
        pz_s[chunk(at)] = value
        so_s[chunk(at)] = sig
        scatter_lanes(mask * sig * value, send_l, at)
        return carry

    steps = [(part * n_step // 2, (part + 1) * n_step // 2) for part in range(2)]
    ex_r = [ToWide(part, send_r, recv_r, part, False) for part in range(2)]
    ex_l = [ToWide(2 + part, send_l, recv_l, part, True) for part in range(2)]
    ex_t = [FromWide(4 + part, tri_s, recv_t, part, True) for part in range(2)]
    ex_dt = [ToWide(6 + part, send_dt, recv_dt, part, True) for part in range(2)]
    ex_dl = [FromWide(8 + part, dl_s, recv_dl, part, True) for part in range(2)]
    ex_dr = [FromWide(10 + part, dr_s, recv_dr, part, False) for part in range(2)]
    lax.fori_loop(*steps[0], project_right, 0)
    pl.semaphore_wait(barrier, n_dev)
    start(ex_r[0])
    lax.fori_loop(*steps[1], project_right, 0)
    start(ex_r[1])
    block_j = cols
    block = block_j * group
    n_block = height // block_j

    def block_rows(at):
        return pl.ds(pl.multiple_of(at * block, block), block)

    def j_rows(at):
        return pl.ds(pl.multiple_of(at * block_j, block_j), block_j)

    late = slice(half_lanes, lanes)
    per_tile = rows // block_j
    halves = [
        [tile_at * per_tile + part * (per_tile // 2) + extra
         for tile_at in range(half_rows) for extra in range(per_tile // 2)]
        for part in range(2)
    ]
    cross_x = [
        cross(0, at, recv_r.at[j_rows(at), late], recv_x.at[j_rows(at), :])
        for at in range(n_block)
    ]
    half_view = slice(0, height // 2)
    for part in range(2):
        lax.fori_loop(*steps[part], project_left, 0)
        if part == 0:
            start(ex_l[0])
        arrived(part, recv_r.at[half_view])
        for at in halves[part]:
            cross_x[at].start()
    start(ex_l[1])

    for load in loads[3:]:
        load.wait()

    @pl.when(my_col < half_cols)
    def _():
        def clear(at, carry):
            recv_dx[at] = jnp.zeros((rows, wide_lanes), jnp.bfloat16)
            return carry

        lax.fori_loop(0, n_dev, clear, 0)

    gain_out = gain_out_ref[...]

    def upstream_part(at, carry):
        gate = jax.nn.sigmoid(dot(normed_s[chunk(at)], w_gate_ref[...]))
        up = up_ref[chunk_rows(at)].reshape(step_pos, chans).astype(jnp.float32)
        weighted = up * gate
        dg_s[chunk(at)] = weighted * (1.0 - gate)
        gq_s[chunk(at)] = dot(weighted.astype(jnp.bfloat16), w_out_ref[...], NT)
        return carry

    row_id = lax.broadcasted_iota(jnp.int32, (block, block_j), 0)
    col_id = lax.broadcasted_iota(jnp.int32, (block, block_j), 1)
    spread = (row_id // group == col_id).astype(jnp.float32).astype(jnp.bfloat16)

    def same(count):
        return (
            lax.broadcasted_iota(jnp.int32, (block, count), 0) % group
            == lax.broadcasted_iota(jnp.int32, (block, count), 1) % group
        )

    def own_lanes(at):
        return pl.ds(pl.multiple_of(half * half_lanes + at * block, block), block)

    def far_lanes(at):
        return pl.ds(pl.multiple_of((1 - half) * half_lanes + at * block, block), block)

    half_tiles = slice(0, n_dev // 2)
    mid = height // 2

    def widen(at, carry):
        wide_rows = dot(spread, recv_r[j_rows(at), :])
        rp_s[block_rows(at), :] = jnp.where(same(lanes), wide_rows, 0.0).astype(jnp.bfloat16)
        return carry

    lax.fori_loop(0, n_block, widen, 0)
    lax.fori_loop(0, n_step, upstream_part, 0)

    def near_triangle(part, step, carry):
        at = (step + my_col) % n_block
        rows_at = slice(part * mid, (part + 1) * mid)
        tri_s[rows_at, own_lanes(at)] = dot(
            recv_l[rows_at, :], rp_s[block_rows(at), :], NT
        ).astype(jnp.bfloat16)
        start_col(ex_t[part], half * half_cols + at)
        return carry

    def widen_far(at, carry):
        wide_rows = dot(spread, recv_x[j_rows(at), :])
        xp_s[block_rows(at), :] = jnp.where(same(half_lanes), wide_rows, 0.0).astype(jnp.bfloat16)
        return carry

    def far_triangle(part, step, carry):
        at = (step + my_col) % n_block
        rows_at = slice(part * mid, (part + 1) * mid)
        tri_s[rows_at, far_lanes(at)] = dot(
            recv_l[rows_at, late], xp_s[block_rows(at), :], NT
        ).astype(jnp.bfloat16)
        start_col(ex_t[part], (1 - half) * half_cols + at)
        return carry

    for part in range(2):
        arrived(2 + part, recv_l.at[half_view])
        lax.fori_loop(0, n_block, functools.partial(near_triangle, part), 0)
        if part == 0:
            for copy in cross_x:
                copy.wait_recv()
            lax.fori_loop(0, n_block, widen_far, 0)
        lax.fori_loop(0, n_block, functools.partial(far_triangle, part), 0)

    def norm_part(at, carry):
        tri = gather_lanes(recv_t, at)
        tnorm, tri_hat, tri_inverse = layer_norm(tri, gain_out)
        tn_s[chunk(at)] = tnorm.astype(jnp.bfloat16)
        d_tri = norm_back(gq_s[chunk(at)], gain_out, tri_hat, tri_inverse)
        scatter_lanes(d_tri, send_dt, at)
        return carry

    for part in range(2):
        arrived(4 + part, recv_t.at[half_tiles])
        lax.fori_loop(*steps[part], norm_part, 0)
        start(ex_dt[part])

    def gate_part(at, carry):
        d_gate = dg_s[chunk(at)] * dot(tn_s[chunk(at)], w_out_ref[...])
        total_s[chunk(at)] = dot(d_gate.astype(jnp.bfloat16), w_gate_ref[...], NT)
        return carry

    def norm_again(at, carry):
        values = pair_ref[chunk_rows(at)].reshape(step_pos, chans).astype(jnp.float32)
        _, scaled, inverse = layer_norm(values, gain_in)
        gq_s[chunk(at)] = scaled
        dg_s[chunk(at)] = jnp.broadcast_to(inverse, scaled.shape)
        return carry

    lax.fori_loop(0, n_step, gate_part, 0)
    for exchange in (*ex_r, *ex_l):
        sent(exchange)
    for copy in cross_x:
        copy.wait_send()

    def far_right_grad(at, carry):
        full = dot(recv_dt[:, far_lanes(at)], recv_l[:, late], TN)
        full = jnp.where(same(half_lanes), full, 0.0).astype(jnp.bfloat16)
        send_dx[j_rows(at), :] = dot(spread, full, TN).astype(jnp.bfloat16)
        return carry

    def far_copy(at, col, part):
        lanes_at = slice(col * wide_lanes, (col + 1) * wide_lanes)
        return pltpu.make_async_remote_copy(
            src_ref=send_dx.at[j_rows(at), lanes_at],
            dst_ref=recv_dx.at[me, part * half_count : (part + 1) * half_count],
            send_sem=far_sem.at[at, col], recv_sem=recv_sem.at[12 + part],
            device_id=((1 - half) * half_rows + at // per_tile, half_cols + col),
            device_id_type=MESH)

    def left_grad(part, step, carry):
        at = (step + my_col) % n_block
        rows_at = slice(part * mid, (part + 1) * mid)
        early = block_rows(at)
        near = recv_dt[rows_at, pl.ds(pl.multiple_of(half * half_lanes, half_lanes), half_lanes)]
        far = recv_dt[
            rows_at, pl.ds(pl.multiple_of((1 - half) * half_lanes, half_lanes), half_lanes)
        ]
        dl_s[rows_at, early] = dot(near, rp_s[:, early]).astype(jnp.bfloat16)
        tail = pl.ds(pl.multiple_of(half_lanes + at * block, block), block)
        dl_s[rows_at, tail] = (dot(near, rp_s[:, tail]) + dot(far, xp_s[:, early])).astype(
            jnp.bfloat16
        )
        start_col(ex_dl[part], at)
        start_col(ex_dl[part], half_cols + at)
        return carry

    def near_right_grad(at, carry):
        full = dot(recv_dt[:, own_lanes(at)], recv_l[...], TN)
        full = jnp.where(same(lanes), full, 0.0).astype(jnp.bfloat16)
        dr_s[j_rows(at), :] = dot(spread, full, TN).astype(jnp.bfloat16)
        return carry

    arrived(6, recv_dt.at[half_view])
    lax.fori_loop(0, n_block, functools.partial(left_grad, 0), 0)
    lax.fori_loop(0, n_step, norm_again, 0)
    arrived(7, recv_dt.at[half_view])

    def far_step(part, step, carry):
        at = step * per_tile + part
        far_right_grad(at, 0)
        for col in range(half_cols):
            far_copy(at, col, part).start()
        return carry

    def near_step(part, step, carry):
        near_right_grad(step * per_tile + part, 0)
        start_row(ex_dr[part], step)
        return carry

    lax.fori_loop(0, n_block, functools.partial(left_grad, 1), 0)
    lax.fori_loop(0, half_rows, functools.partial(far_step, 0), 0)
    lax.fori_loop(0, half_rows, functools.partial(far_step, 1), 0)
    lax.fori_loop(0, half_rows, functools.partial(near_step, 0), 0)
    lax.fori_loop(0, half_rows, functools.partial(near_step, 1), 0)

    def finish_left(at, carry):
        d_left = gather_lanes(recv_dl, at) * mask
        sig = so_s[chunk(at)]
        d_zero = d_left * sig
        d_one = d_zero * pz_s[chunk(at)] * (1.0 - sig)
        total = total_s[chunk(at)]
        total = total + dot(d_zero.astype(jnp.bfloat16), w_proj_ref[:, 0:chans], NT)
        total = total + dot(d_one.astype(jnp.bfloat16), w_proj_ref[:, chans : 2 * chans], NT)
        total_s[chunk(at)] = total
        return carry

    for part in range(2):
        arrived(8 + part, recv_dl.at[half_tiles])
        lax.fori_loop(*steps[part], finish_left, 0)
    for exchange in (*ex_t, *ex_dt, *ex_dl):
        sent(exchange)

    def far_sent(at, carry):
        for col in range(half_cols):
            far_copy(at, col, 0).wait_send()
        return carry

    lax.fori_loop(0, n_block, far_sent, 0)

    def out_copy(at):
        return pltpu.make_async_copy(
            pair_ref.at[chunk_rows(at)], out_ref.at[chunk_rows(at)], out_sem.at[at]
        )

    def finish_right(at, carry):
        total = total_s[chunk(at)]
        d_right = gather_lanes(recv_dr, at, recv_dx) * mask
        sig = st_s[chunk(at)]
        d_two = d_right * sig
        d_three = d_two * pt_s[chunk(at)] * (1.0 - sig)
        total = total + dot(d_two.astype(jnp.bfloat16), w_proj_ref[:, 2 * chans : 3 * chans], NT)
        total = total + dot(d_three.astype(jnp.bfloat16), w_proj_ref[:, 3 * chans : 4 * chans], NT)
        scaled, inverse = gq_s[chunk(at)], dg_s[chunk(at)]
        result = norm_back(total, gain_in, scaled, inverse).astype(jnp.bfloat16)
        pair_ref[chunk_rows(at)] = result.reshape(STEP_ROWS, cols, chans)
        out_copy(at).start()
        return carry

    for part in range(2):
        arrived(10 + part, recv_dr.at[half_tiles])

        @pl.when(my_col >= half_cols)
        def _():
            arrived(12 + part, recv_dx.at[half_tiles])

        lax.fori_loop(*steps[part], finish_right, 0)
    for exchange in ex_dr:
        sent(exchange)
    for at in range(n_step):
        out_copy(at).wait()


def spread_channels(sizes, pair, grad_out, keep, w_proj, w_gate, w_out, gain_in, gain_out):
    n_row, n_col, rows, cols, chans, group = sizes
    n_dev = n_row // 2 * n_col
    pos = rows * cols
    step_pos = STEP_ROWS * cols
    wide_lanes = cols * group
    height, lanes = n_row // 2 * rows, n_col * wide_lanes
    low, full = jnp.bfloat16, jnp.float32
    hbm = pl.BlockSpec(memory_space=pltpu.HBM)
    flat_low = pltpu.VMEM((pos, chans), low)
    flat = pltpu.VMEM((pos, chans), full)
    tiles = pltpu.VMEM((n_dev, rows, wide_lanes), low)
    whole = pltpu.VMEM((height, lanes), low)
    part = pltpu.VMEM((height, lanes // 2), low)
    operands = (
        pair, grad_out, w_proj, w_gate, w_out, gain_in.reshape(1, chans), gain_out.reshape(1, chans)
    )
    return pl.pallas_call(
        functools.partial(kernel, sizes),
        out_shape=jax.ShapeDtypeStruct(pair.shape, low),
        in_specs=[pl.BlockSpec(memory_space=pltpu.SMEM)] + [hbm] * 7,
        out_specs=pl.BlockSpec(memory_space=pl.ANY),
        scratch_shapes=[pltpu.VMEM(item.shape, item.dtype) for item in operands]
        + [
            flat_low, flat, flat, flat, flat, flat, flat, flat_low, flat,
            pltpu.VMEM((step_pos, chans), full),
            tiles, tiles, whole, whole, part,
            pltpu.VMEM((height * group, lanes), low),
            pltpu.VMEM((height * group, lanes // 2), low),
            whole, tiles, tiles, whole, part, tiles, whole, whole, tiles, tiles,
            pltpu.SemaphoreType.DMA((7,)),
            pltpu.SemaphoreType.DMA((12, n_dev)),
            pltpu.SemaphoreType.DMA((14,)),
            pltpu.SemaphoreType.DMA((2, height // cols)),
            pltpu.SemaphoreType.DMA((height // cols, n_col // 2)),
            pltpu.SemaphoreType.DMA((rows // STEP_ROWS,)),
        ],
        compiler_params=pltpu.CompilerParams(
            collective_id=0, has_side_effects=True, vmem_limit_bytes=56 * 2**20
        ),
    )(keep, *operands)


def tile_body(n_row, n_col, pair, grad_out, keep, *rest):
    rows, cols, chans = pair.shape
    n_dev = n_row // 2 * n_col
    group = chans // n_dev
    fits = (
        keep.shape[0] == 2
        and n_row % 2 == 0
        and n_col % 2 == 0
        and n_row * rows == 2 * BS
        and n_col * cols == 2 * BS
        and group * n_dev == chans
        and cols % n_dev == 0
        and rows == 2 * cols
        and rows % (2 * STEP_ROWS) == 0
    )
    if fits:
        sizes = (n_row, n_col, rows, cols, chans, group)
        return spread_channels(sizes, pair, grad_out, keep, *rest)
    return on_device(pair, grad_out, keep, *rest)


def solution(mesh):
    return jax.shard_map(
        functools.partial(tile_body, mesh.shape["row"], mesh.shape["col"]),
        mesh=mesh,
        in_specs=(P("row", "col", None), P("row", "col", None), P(), P(), P(), P(), P(), P()),
        out_specs=P("row", "col", None),
        check_vma=False,
    )
```
